32 devices in a mesh: item: 8 (over z, y), seq: 4 (over x, core).
Axes of the slice: x: 2, y: 2, z: 4, core: 2. Of those that a mesh axis runs over, the one named last changes fastest.
Arguments:
- tokens: bfloat16 [64, 1024, 1280], P('item', 'seq'), may hold values from -6 to 6
- lengths: int32 [64], P('item'), may hold values from 30 to 1024, as said below
- entry_gain: float32 [1280], replicated, may hold values from 0.25 to 1.75
- entry_shift: float32 [1280], replicated, may hold values from -1.5 to 1.5
- narrow_weight: bfloat16 [1280, 640], replicated, may hold values from -0.15625 to 0.15625
- narrow_bias: float32 [640], replicated, may hold values from -1.5 to 1.5
- middle_gain: float32 [640], replicated, may hold values from 0.25 to 1.75
- middle_shift: float32 [640], replicated, may hold values from -1.5 to 1.5
- dilated_weight: bfloat16 [5, 640, 640], replicated, may hold values from -0.109375 to 0.109375
- dilated_bias: float32 [640], replicated, may hold values from -1.5 to 1.5
- final_gain: float32 [640], replicated, may hold values from 0.25 to 1.75
- final_shift: float32 [640], replicated, may hold values from -1.5 to 1.5
- widen_weight: bfloat16 [640, 1280], replicated, may hold values from -0.25 to 0.25
- widen_bias: float32 [1280], replicated, may hold values from -1.5 to 1.5
- out_cotangent: bfloat16 [64, 1024, 1280], P('item', 'seq'), may hold values from -6 to 6
Outputs:
- block_out: bfloat16 [64, 1024, 1280], P('item', 'seq')
- tokens_grad: bfloat16 [64, 1024, 1280], P('item', 'seq')
- entry_gain_grad: float32 [1280], replicated
- entry_shift_grad: float32 [1280], replicated
- narrow_weight_grad: float32 [1280, 640], replicated
- narrow_bias_grad: float32 [640], replicated
- middle_gain_grad: float32 [640], replicated
- middle_shift_grad: float32 [640], replicated
- dilated_weight_grad: float32 [5, 640, 640], replicated
- dilated_bias_grad: float32 [640], replicated
- final_gain_grad: float32 [640], replicated
- final_shift_grad: float32 [640], replicated
- widen_weight_grad: float32 [640, 1280], replicated
- widen_bias_grad: float32 [1280], replicated
The draws below stay inside these ranges and needn't reach their ends.
Inputs may be any that keep to these rules, and one draw needn't show every extreme that they name: `lengths`: protein 0 has 1024 residues and protein 1 has 30; the others are mostly short.
All inputs are finite; a program needn't handle non-finite values.
Results may differ from the reference program's by a relative error of at most 0.0072.
Values may be sent and summed in bfloat16 or wider, within the bound.
No kernel may reach another device: no remote copies, remote signals or barrier semaphores. Data moves between devices by JAX's collectives and lax.ppermute only.
A program may use at most 256 MiB of HBM per device.

```python
import jax
import jax.numpy as jnp
from jax import lax

D = 1280
INNER = 640
KERNEL_TAPS = 5
DILATION_SIZE = 64
PADDED_LENGTH = 1024
MIN_LEN = 30
PROTEINS = 64


def draw_lengths(key, part):
    picks = jax.random.randint(jax.random.fold_in(key, 11), (PROTEINS, 3), 0, PADDED_LENGTH - MIN_LEN + 1)
    sizes = MIN_LEN + jnp.min(picks, axis=1)
    sizes = jnp.minimum(sizes, PADDED_LENGTH)
    sizes = sizes.at[0].set(PADDED_LENGTH)
    sizes = sizes.at[1].set(MIN_LEN)
    return sizes.astype(jnp.int32)


def block_levels(own_key, extent, split, low, high):
    def one(dim, shards_of):
        heights = jax.random.uniform(jax.random.fold_in(jax.random.fold_in(own_key, 6), dim), (shards_of,), jnp.float32, low / len(split), high / len(split))
        return jnp.repeat(jnp.exp(heights), extent[dim] // shards_of).reshape((-1,) + (1,) * (len(extent) - dim - 1))

    loudness = one(*split[0])
    for cut in split[1:]:
        loudness = loudness * one(*cut)
    return loudness


def noise(own_key, shape, deviation, reach, shards=(), kind=jnp.bfloat16):
    loudness = block_levels(own_key, shape, shards, -0.22, 0.18) if shards else 1.0
    drawn = jax.random.normal(own_key, shape, jnp.float32) * deviation * loudness
    return jnp.minimum(jnp.maximum(drawn, -reach), reach).astype(kind)


def setup_inputs(seed: int = 0) -> dict:
    key_list = jax.random.split(jax.random.key(seed), 16)
    return {
        "tokens": noise(key_list[0], (PROTEINS, PADDED_LENGTH, D), 1.0, 6.0, ((0, 8), (1, 4))),
        "lengths": draw_lengths(jax.random.fold_in(key_list[15], 71), 0),
        "entry_gain": jnp.clip(1.0 + 0.15 * jax.random.normal(key_list[2], (D,), jnp.float32), 0.25, 1.75),
        "entry_shift": noise(key_list[3], (D,), 0.3, 1.5, (), jnp.float32),
        "narrow_weight": noise(key_list[4], (D, INNER), D ** -0.5, 0.15625),
        "narrow_bias": noise(key_list[5], (INNER,), 0.3, 1.5, (), jnp.float32),
        "middle_gain": jnp.clip(1.0 + 0.15 * jax.random.normal(key_list[6], (INNER,), jnp.float32), 0.25, 1.75),
        "middle_shift": noise(key_list[7], (INNER,), 0.3, 1.5, (), jnp.float32),
        "dilated_weight": noise(key_list[8], (KERNEL_TAPS, INNER, INNER), (KERNEL_TAPS * INNER) ** -0.5, 0.109375),
        "dilated_bias": noise(key_list[9], (INNER,), 0.3, 1.5, (), jnp.float32),
        "final_gain": jnp.clip(1.0 + 0.15 * jax.random.normal(key_list[10], (INNER,), jnp.float32), 0.25, 1.75),
        "final_shift": noise(key_list[11], (INNER,), 0.3, 1.5, (), jnp.float32),
        "widen_weight": noise(key_list[12], (INNER, D), INNER ** -0.5, 0.25),
        "widen_bias": noise(key_list[13], (D,), 0.3, 1.5, (), jnp.float32),
        "out_cotangent": noise(key_list[14], (PROTEINS, PADDED_LENGTH, D), 1.0, 6.0, ((0, 8), (1, 4))),
    }


@jax.custom_vjp
def low(v):
    return lax.optimization_barrier(v.astype(jnp.bfloat16)).astype(jnp.float32)

@jax.custom_vjp
def low_back(v):
    return v

def low_keep(v):
    return (low(v), None)

def low_pass(kept, grad):
    return (grad,)

def back_keep(v):
    return (v, None)

def back_low(kept, grad):
    return (low(grad),)
low.defvjp(low_keep, low_pass)
low_back.defvjp(back_keep, back_low)
EPS = 1e-05
HIGH_PRECISION = lax.Precision.HIGHEST

def normalize(values, gain, shift):
    mean = lax.optimization_barrier(jnp.mean(values, axis=-1, keepdims=True))
    centred = values - mean
    spread = lax.optimization_barrier(jnp.mean(centred * centred, axis=-1, keepdims=True))
    return centred * lax.rsqrt(spread + EPS) * gain + shift

def activate(values, gain, shift, keep):
    return jax.nn.gelu(normalize(values, gain, shift), approximate=False) * keep

def forward(source, keep, parameters):
    entry_scale, entry_bias, narrow_matrix, narrow_channels, middle_scale, middle_bias, dilated_matrix, dilated_channels, final_scale, final_bias, widen_matrix, widen_channels = parameters
    receptive_reach = (KERNEL_TAPS - 1) // 2 * DILATION_SIZE
    first = low(activate(source, entry_scale, entry_bias, keep))
    narrow = low_back(jnp.dot(first, narrow_matrix, precision=HIGH_PRECISION) + narrow_channels)
    second = low(activate(narrow, middle_scale, middle_bias, keep))
    padded_input = jnp.pad(second, ((0, 0), (receptive_reach, receptive_reach), (0, 0)))
    mixed_output = dilated_channels
    for tap_index in range(KERNEL_TAPS):
        mixed_output = mixed_output + jnp.dot(padded_input[:, tap_index * DILATION_SIZE:tap_index * DILATION_SIZE + PADDED_LENGTH], dilated_matrix[tap_index], precision=HIGH_PRECISION)
    mixed_output = low_back(mixed_output)
    third = low(activate(mixed_output, final_scale, final_bias, keep))
    widened = low_back(jnp.dot(third, widen_matrix, precision=HIGH_PRECISION) + widen_channels)
    return source + widened

def reference(tokens, lengths, entry_gain, entry_shift, narrow_weight, narrow_bias, middle_gain, middle_shift, dilated_weight, dilated_bias, final_gain, final_shift, widen_weight, widen_bias, out_cotangent):
    group = 4
    blocks = PROTEINS // group
    parameters = tuple((p.astype(jnp.float32) for p in (entry_gain, entry_shift, narrow_weight, narrow_bias, middle_gain, middle_shift, dilated_weight, dilated_bias, final_gain, final_shift, widen_weight, widen_bias)))
    places = jnp.arange(PADDED_LENGTH, dtype=jnp.int32)

    def step(totals, items):
        source_in, sizes, upstream = items
        keep = (places[None, :] < sizes[:, None]).astype(jnp.float32)[:, :, None]
        result, pull = jax.vjp(lambda s, p: forward(s, keep, p), source_in.astype(jnp.float32), parameters)
        grad_source, grad_params = pull(upstream.astype(jnp.float32))
        totals = tuple((a + b for a, b in zip(totals, grad_params)))
        return (totals, (result.astype(jnp.bfloat16), grad_source.astype(jnp.bfloat16)))
    zeros = tuple((jnp.zeros_like(p) for p in parameters))
    inputs = (tokens.reshape(blocks, group, PADDED_LENGTH, D), lengths.reshape(blocks, group).astype(jnp.int32), out_cotangent.reshape(blocks, group, PADDED_LENGTH, D))
    totals, (outputs, grads) = lax.scan(step, zeros, inputs)
    return (outputs.reshape(PROTEINS, PADDED_LENGTH, D), grads.reshape(PROTEINS, PADDED_LENGTH, D), totals[0], totals[1], totals[2], totals[3], totals[4], totals[5], totals[6], totals[7], totals[8], totals[9], totals[10], totals[11])
```

```python
import functools

import jax
import jax.numpy as jnp
from jax import lax
from jax.experimental import pallas as pl
from jax.experimental.pallas import tpu as pltpu
from jax.sharding import PartitionSpec as P

DILATION_SIZE = 64
EPS = 1e-05
BF = jnp.bfloat16
F32 = jnp.float32
ROWS = 16
VMEM = 60 << 20


def gelu_parts(y):
    size = jnp.abs(y)
    t = 1.0 / (1.0 + (0.3275911 * 0.7071067811865476) * size)
    bell = jnp.exp(-0.5 * y * y)
    poly = 1.061405429 * 0.5
    for c in (-1.453152027, 1.421413741, -0.284496736, 0.254829592):
        poly = poly * t + c * 0.5
    tail = poly * t * bell
    cdf = jnp.where(y >= 0, 1.0 - tail, tail)
    return cdf, y * bell * 0.3989422804014327


def norm_stats(v):
    mean = jnp.mean(v, axis=-1, keepdims=True)
    c = v - mean
    r = lax.rsqrt(jnp.mean(c * c, axis=-1, keepdims=True) + EPS)
    return c * r, r


def keep_rows(i, limit, rows):
    at = i * rows + lax.broadcasted_iota(jnp.int32, (rows, 1), 0)
    return at < limit


def fold(v):
    return jnp.sum(v.reshape(-1, 8, v.shape[-1]), axis=0)


def entry_kernel(limits, tok, g1, b1, wn, bn, g2, b2, first, n1, gp1, r1, second, n2, gp2, r2, narrow):
    limit = limits[pl.program_id(0)]
    span = tok.shape[1]

    def one(i, _):
        s = pl.ds(i * ROWS, ROWS)
        keep = keep_rows(i, limit, ROWS)
        n, r = norm_stats(tok[0, s, :].astype(F32))
        y = n * g1[...] + b1[...]
        cdf, bell = gelu_parts(y)
        first[0, s, :] = jnp.where(keep, y * cdf, 0.0).astype(BF)
        gp1[0, s, :] = jnp.where(keep, cdf + bell, 0.0).astype(BF)
        n1[0, s, :] = n.astype(BF)
        r1[0, s, :] = jnp.broadcast_to(r, (ROWS, 128))
        return 0

    lax.fori_loop(0, span // ROWS, one, 0, unroll=2)
    narrow[...] = jnp.dot(first[0], wn[...], preferred_element_type=F32) + bn[...]

    def two(i, _):
        s = pl.ds(i * ROWS, ROWS)
        keep = keep_rows(i, limit, ROWS)
        n, r = norm_stats(narrow[s, :])
        y = n * g2[...] + b2[...]
        cdf, bell = gelu_parts(y)
        second[0, s, :] = jnp.where(keep, y * cdf, 0.0).astype(BF)
        gp2[0, s, :] = jnp.where(keep, cdf + bell, 0.0).astype(BF)
        n2[0, s, :] = n.astype(BF)
        r2[0, s, :] = jnp.broadcast_to(r, (ROWS, 128))
        return 0

    lax.fori_loop(0, span // ROWS, two, 0, unroll=2)


def dot_nt(a, b):
    return lax.dot_general(a, b, (((1,), (1,)), ((), ())), preferred_element_type=F32)


def dot_tn(a, b):
    return lax.dot_general(a, b, (((0,), (0,)), ((), ())), preferred_element_type=F32)


def middle_kernel(limits, tok, cot, own, before, after, wd, bd, g3, b3, ww, bw,
                  out, gm, dww, dwd, vecs, wsum, pad, mixed, third, n3, gp3, r3, gt):
    step = pl.program_id(0)
    taps = wd.shape[0]
    reach = before.shape[1]
    span = tok.shape[1]
    inner = wd.shape[1]
    limit = limits[step]

    @pl.when(step == 0)
    def _():
        dww[...] = jnp.zeros_like(dww)
        dwd[...] = jnp.zeros_like(dwd)
        vecs[...] = jnp.zeros_like(vecs)
        wsum[...] = jnp.zeros_like(wsum)

    pad[:reach] = before[0]
    pad[reach : reach + span] = own[0]
    pad[reach + span :] = after[0]
    acc = bd[...]
    for k in range(taps):
        acc = acc + jnp.dot(pad[k * DILATION_SIZE : k * DILATION_SIZE + span], wd[k], preferred_element_type=F32)
    mixed[...] = acc

    def one(i, _):
        s = pl.ds(i * ROWS, ROWS)
        keep = keep_rows(i, limit, ROWS)
        n, r = norm_stats(mixed[s, :])
        y = n * g3[...] + b3[...]
        cdf, bell = gelu_parts(y)
        third[s, :] = jnp.where(keep, y * cdf, 0.0).astype(BF)
        gp3[s, :] = jnp.where(keep, cdf + bell, 0.0)
        n3[s, :] = n
        r3[s, :] = jnp.broadcast_to(r, (ROWS, 128))
        return 0

    lax.fori_loop(0, span // ROWS, one, 0, unroll=2)
    widened = jnp.dot(third[...], ww[...], preferred_element_type=F32) + bw[...]
    out[0] = (tok[0].astype(F32) + widened).astype(BF)
    wsum[...] += fold(cot[0].astype(F32))
    dww[...] += dot_tn(third[...], cot[0])
    gt[...] = dot_nt(cot[0], ww[...])

    def two(i, carry):
        gain, shift, bias = carry
        s = pl.ds(i * ROWS, ROWS)
        grad = gt[s, :] * gp3[s, :]
        n = n3[s, :]
        gn = grad * n
        h = grad * g3[...]
        hn = h * n
        d = r3[s, 0:1] * (h - jnp.mean(h, axis=-1, keepdims=True) - n * jnp.mean(hn, axis=-1, keepdims=True))
        low = d.astype(BF)
        gm[0, s, :] = low
        return gain + fold(gn), shift + fold(grad), bias + fold(low.astype(F32))

    zero = jnp.zeros((8, inner), F32)
    gain, shift, bias = lax.fori_loop(0, span // ROWS, two, (zero, zero, zero), unroll=2)
    vecs[0] += gain
    vecs[1] += shift
    vecs[2] += bias
    for k in range(taps):
        dwd[k] += dot_tn(pad[k * DILATION_SIZE : k * DILATION_SIZE + span], gm[0])


def exit_kernel(limits, gm, before, after, wd, n2, gp2, r2, g2, first, n1, gp1, r1, g1, cot, wn,
                out, dwn, vecs, evecs, pad, gs, gnl, gf):
    step = pl.program_id(0)
    taps = wd.shape[0]
    reach = before.shape[1]
    span = gm.shape[1]
    inner = wd.shape[1]

    @pl.when(step == 0)
    def _():
        dwn[...] = jnp.zeros_like(dwn)
        vecs[...] = jnp.zeros_like(vecs)
        evecs[...] = jnp.zeros_like(evecs)

    pad[:reach] = before[0]
    pad[reach : reach + span] = gm[0]
    pad[reach + span :] = after[0]
    acc = None
    for k in range(taps):
        at = (taps - 1 - k) * DILATION_SIZE
        term = dot_nt(pad[at : at + span], wd[k])
        acc = term if acc is None else acc + term
    gs[...] = acc

    def one(i, carry):
        gain, shift, bias = carry
        s = pl.ds(i * ROWS, ROWS)
        grad = gs[s, :] * gp2[0, s, :].astype(F32)
        n = n2[0, s, :].astype(F32)
        h = grad * g2[...]
        d = r2[0, s, 0:1] * (
            h - jnp.mean(h, axis=-1, keepdims=True) - n * jnp.mean(h * n, axis=-1, keepdims=True)
        )
        low = d.astype(BF)
        gnl[s, :] = low
        return gain + fold(grad * n), shift + fold(grad), bias + fold(low.astype(F32))

    zero = jnp.zeros((8, inner), F32)
    gain, shift, bias = lax.fori_loop(0, span // ROWS, one, (zero, zero, zero), unroll=2)
    vecs[0] += gain
    vecs[1] += shift
    vecs[2] += bias
    dwn[...] += dot_tn(first[0], gnl[...])
    gf[...] = dot_nt(gnl[...], wn[...])

    def two(i, _):
        s = pl.ds(i * ROWS, ROWS)
        grad = gf[s, :] * gp1[0, s, :].astype(F32)
        n = n1[0, s, :].astype(F32)
        h = grad * g1[...]
        d = r1[0, s, 0:1] * (
            h - jnp.mean(h, axis=-1, keepdims=True) - n * jnp.mean(h * n, axis=-1, keepdims=True)
        )
        out[0, s, :] = (cot[0, s, :].astype(F32) + d).astype(BF)
        evecs[0] += fold(grad * n)
        evecs[1] += fold(grad)
        return 0

    lax.fori_loop(0, span // ROWS, two, 0, unroll=2)


def call(body, name, seqs, scalars, ins, outs, scratch, flops=0, nbytes=0):
    def spec(shape, each):
        rest = (0,) * (len(shape) - 1)
        if each:
            return pl.BlockSpec((1,) + tuple(shape[1:]), lambda i, *_: (i,) + rest)
        return pl.BlockSpec(tuple(shape), lambda i, *_: (0,) + rest)

    return pl.pallas_call(
        body,
        name=name,
        grid_spec=pltpu.PrefetchScalarGridSpec(
            num_scalar_prefetch=1,
            grid=(seqs,),
            in_specs=[spec(a.shape, e) for a, e in ins],
            out_specs=[spec(s, e) for s, _, e in outs],
            scratch_shapes=[pltpu.VMEM(s, d) for s, d in scratch],
        ),
        out_shape=[jax.ShapeDtypeStruct(s, d) for s, d, _ in outs],
        compiler_params=pltpu.CompilerParams(vmem_limit_bytes=VMEM),
        cost_estimate=pl.CostEstimate(flops=flops, transcendentals=0, bytes_accessed=nbytes),
    )(scalars, *[a for a, _ in ins])


def halo(cells, width):
    count = lax.axis_size("seq")
    ends = count - 1
    before = lax.ppermute(cells[:, cells.shape[1] - width :], "seq", [(i, i + 1) for i in range(ends)])
    after = lax.ppermute(cells[:, :width], "seq", [(i + 1, i) for i in range(ends)])
    return before, after


def reduce_all(groups):
    return [lax.psum(g.astype(BF), ("item", "seq")).astype(F32) for g in groups]


def on_device(tokens, lengths, entry_gain, entry_shift, narrow_weight, narrow_bias, middle_gain, middle_shift,
              dilated_weight, dilated_bias, final_gain, final_shift, widen_weight, widen_bias, out_cotangent):
    seqs, span, width = tokens.shape
    taps, inner, _ = dilated_weight.shape
    reach = (taps - 1) // 2 * DILATION_SIZE
    limits = lengths - lax.axis_index("seq").astype(jnp.int32) * span

    def row(v):
        return v.reshape(1, -1)

    wide = (seqs, span, width)
    slim = (seqs, span, inner)
    stat = (seqs, span, 128)
    rows = seqs * span
    first, n1, gp1, r1, second, n2, gp2, r2 = call(
        entry_kernel, "entry", seqs, limits,
        [(tokens, True), (row(entry_gain), False), (row(entry_shift), False), (narrow_weight, False),
         (row(narrow_bias), False), (row(middle_gain), False), (row(middle_shift), False)],
        [(wide, BF, True), (wide, BF, True), (wide, BF, True), (stat, F32, True),
         (slim, BF, True), (slim, BF, True), (slim, BF, True), (stat, F32, True)],
        [((span, inner), F32)],
        flops=16 * rows * width * inner, nbytes=rows * width * 12,
    )
    before, after = halo(second, reach)
    out, gm, dww, dwd, vecs3, wsum = call(
        middle_kernel, "middle", seqs, limits,
        [(tokens, True), (out_cotangent, True), (second, True), (before, True), (after, True),
         (dilated_weight, False), (row(dilated_bias), False), (row(final_gain), False), (row(final_shift), False),
         (widen_weight, False), (row(widen_bias), False)],
        [(wide, BF, True), (slim, BF, True), ((inner, width), F32, False), ((taps, inner, inner), F32, False),
         ((3, 8, inner), F32, False), ((8, width), F32, False)],
        [((span + 2 * reach, inner), BF), ((span, inner), F32), ((span, inner), BF), ((span, inner), F32),
         ((span, inner), F32), ((span, 128), F32), ((span, inner), F32)],
        flops=16 * rows * width * inner, nbytes=rows * width * 12,
    )
    gbefore, gafter = halo(gm, reach)
    tokens_grad, dwn, vecs2, evecs = call(
        exit_kernel, "exit", seqs, limits,
        [(gm, True), (gbefore, True), (gafter, True), (dilated_weight, False), (n2, True), (gp2, True), (r2, True),
         (row(middle_gain), False), (first, True), (n1, True), (gp1, True), (r1, True), (row(entry_gain), False),
         (out_cotangent, True), (narrow_weight, False)],
        [(wide, BF, True), ((width, inner), F32, False), ((3, 8, inner), F32, False), ((2, 8, width), F32, False)],
        [((span + 2 * reach, inner), BF), ((span, inner), F32), ((span, inner), BF), ((span, width), F32)],
        flops=12 * rows * width * inner, nbytes=rows * width * 12,
    )
    small = jnp.concatenate(
        [evecs.sum(1).reshape(-1), wsum.sum(0), vecs2.sum(1).reshape(-1), vecs3.sum(1).reshape(-1)]
    )
    small = lax.psum(small, ("item", "seq"))
    eg, es, wb = (small[i * width : (i + 1) * width] for i in range(3))
    mg, ms, nb, fg, fs, db = (small[3 * width + i * inner : 3 * width + (i + 1) * inner] for i in range(6))
    sww, swd, swn = reduce_all([dww, dwd, dwn])
    return (out, tokens_grad, eg, es, swn, nb, mg, ms, swd, db, fg, fs, sww, wb)


def solution(mesh):
    split = P("item", "seq", None)
    in_specs = (split, P("item")) + (P(),) * 12 + (split,)
    out_specs = (split, split) + (P(),) * 12
    return jax.shard_map(on_device, mesh=mesh, in_specs=in_specs, out_specs=out_specs, check_vma=False)
```

```python
import jax
import jax.numpy as jnp
from jax import lax
from jax.experimental import pallas as pl
from jax.experimental.pallas import tpu as pltpu
from jax.sharding import PartitionSpec as P

DILATION_SIZE = 64
EPS = 1e-05
BF = jnp.bfloat16
F32 = jnp.float32
ROWS = 16
VMEM = 60 << 20


def gelu_parts(y):
    size = jnp.abs(y)
    t = 1.0 / (1.0 + (0.3275911 * 0.7071067811865476) * size)
    bell = jnp.exp(-0.5 * y * y)
    poly = 1.061405429 * 0.5
    for c in (-1.453152027, 1.421413741, -0.284496736, 0.254829592):
        poly = poly * t + c * 0.5
    tail = poly * t * bell
    cdf = jnp.where(y >= 0, 1.0 - tail, tail)
    return cdf, y * bell * 0.3989422804014327


def norm_stats(v):
    mean = jnp.mean(v, axis=-1, keepdims=True)
    c = v - mean
    r = lax.rsqrt(jnp.mean(c * c, axis=-1, keepdims=True) + EPS)
    return c * r, r


def keep_rows(i, limit, rows):
    at = i * rows + lax.broadcasted_iota(jnp.int32, (rows, 1), 0)
    return at < limit


def fold(v):
    return jnp.sum(v.reshape(-1, 8, v.shape[-1]), axis=0)


def entry_kernel(limits, tok, g1, b1, wn, bn, g2, b2, first, n1, gp1, r1, second, n2, gp2, r2, narrow):
    limit = limits[pl.program_id(0)]
    span = tok.shape[1]

    def one(i, _):
        s = pl.ds(i * ROWS, ROWS)
        keep = keep_rows(i, limit, ROWS)
        n, r = norm_stats(tok[0, s, :].astype(F32))
        y = n * g1[...] + b1[...]
        cdf, bell = gelu_parts(y)
        first[0, s, :] = jnp.where(keep, y * cdf, 0.0).astype(BF)
        gp1[0, s, :] = jnp.where(keep, cdf + bell, 0.0).astype(BF)
        n1[0, s, :] = n.astype(BF)
        r1[0, s, :] = jnp.broadcast_to(r, (ROWS, 128))
        return 0

    lax.fori_loop(0, span // ROWS, one, 0, unroll=2)
    narrow[...] = jnp.dot(first[0], wn[...], preferred_element_type=F32) + bn[...]

    def two(i, _):
        s = pl.ds(i * ROWS, ROWS)
        keep = keep_rows(i, limit, ROWS)
        n, r = norm_stats(narrow[s, :])
        y = n * g2[...] + b2[...]
        cdf, bell = gelu_parts(y)
        second[0, s, :] = jnp.where(keep, y * cdf, 0.0).astype(BF)
        gp2[0, s, :] = jnp.where(keep, cdf + bell, 0.0).astype(BF)
        n2[0, s, :] = n.astype(BF)
        r2[0, s, :] = jnp.broadcast_to(r, (ROWS, 128))
        return 0

    lax.fori_loop(0, span // ROWS, two, 0, unroll=2)


def dot_nt(a, b):
    return lax.dot_general(a, b, (((1,), (1,)), ((), ())), preferred_element_type=F32)


def dot_tn(a, b):
    return lax.dot_general(a, b, (((0,), (0,)), ((), ())), preferred_element_type=F32)


def middle_kernel(limits, tok, cot, own, before, after, wd, bd, g3, b3, ww, bw,
                  out, gm, keep_a, send_a, keep_b, send_b, vecs, wsum, dww, dwd, pad, mixed, third, n3, gp3, r3, gt):
    step = pl.program_id(0)
    taps = wd.shape[0]
    reach = before.shape[1]
    span = tok.shape[1]
    inner = wd.shape[1]
    limit = limits[step]

    @pl.when(step == 0)
    def _():
        dww[...] = jnp.zeros_like(dww)
        dwd[...] = jnp.zeros_like(dwd)
        vecs[...] = jnp.zeros_like(vecs)
        wsum[...] = jnp.zeros_like(wsum)

    pad[:reach] = before[0]
    pad[reach : reach + span] = own[0]
    pad[reach + span :] = after[0]
    acc = bd[...]
    for k in range(taps):
        acc = acc + jnp.dot(pad[k * DILATION_SIZE : k * DILATION_SIZE + span], wd[k], preferred_element_type=F32)
    mixed[...] = acc

    def one(i, _):
        s = pl.ds(i * ROWS, ROWS)
        keep = keep_rows(i, limit, ROWS)
        n, r = norm_stats(mixed[s, :])
        y = n * g3[...] + b3[...]
        cdf, bell = gelu_parts(y)
        third[s, :] = jnp.where(keep, y * cdf, 0.0).astype(BF)
        gp3[s, :] = jnp.where(keep, cdf + bell, 0.0)
        n3[s, :] = n
        r3[s, :] = jnp.broadcast_to(r, (ROWS, 128))
        return 0

    lax.fori_loop(0, span // ROWS, one, 0, unroll=2)
    widened = jnp.dot(third[...], ww[...], preferred_element_type=F32) + bw[...]
    out[0] = (tok[0].astype(F32) + widened).astype(BF)
    wsum[...] += fold(cot[0].astype(F32))
    dww[...] += dot_tn(third[...], cot[0])
    gt[...] = dot_nt(cot[0], ww[...])

    def two(i, carry):
        gain, shift, bias = carry
        s = pl.ds(i * ROWS, ROWS)
        grad = gt[s, :] * gp3[s, :]
        n = n3[s, :]
        gn = grad * n
        h = grad * g3[...]
        hn = h * n
        d = r3[s, 0:1] * (h - jnp.mean(h, axis=-1, keepdims=True) - n * jnp.mean(hn, axis=-1, keepdims=True))
        low = d.astype(BF)
        gm[0, s, :] = low
        return gain + fold(gn), shift + fold(grad), bias + fold(low.astype(F32))

    zero = jnp.zeros((8, inner), F32)
    gain, shift, bias = lax.fori_loop(0, span // ROWS, two, (zero, zero, zero), unroll=2)
    vecs[0] += gain
    vecs[1] += shift
    vecs[2] += bias
    for k in range(taps):
        dwd[k * inner : (k + 1) * inner] += dot_tn(pad[k * DILATION_SIZE : k * DILATION_SIZE + span], gm[0])

    @pl.when(step == pl.num_programs(0) - 1)
    def _():
        cut = split_rows(taps * inner)
        deal((dww.at[:, :inner], dwd.at[:cut]), limits[limits.shape[0] - 1], keep_a, send_a)
        deal((dww.at[:, inner:], dwd.at[cut:]), limits[limits.shape[0] - 1], keep_b, send_b)


def split_rows(rows):
    return rows // 2 // 128 * 128


def deal(parts, bit, keep, send):
    half = keep.shape[0]

    def put(chosen, target, kind):
        at = 0
        for part in parts:
            low, high = max(at, chosen * half), min(at + part.shape[0], (chosen + 1) * half)
            if low < high:
                target[low - chosen * half : high - chosen * half] = part[low - at : high - at].astype(kind)
            at += part.shape[0]

    for value in (0, 1):

        @pl.when(bit == value)
        def _():
            put(value, keep, F32)
            put(1 - value, send, BF)


def back_kernel(limits, gm, before, after, wd, n2, gp2, r2, g2, first, *refs):
    if len(refs) == 5:
        gnl, vecs, dwn, pad, gs = refs
        begun = None
    else:
        begun, vecs_begun, gnl, vecs, keep_a, send_a, keep_b, send_b, dwn, pad, gs = refs
    step = pl.program_id(0)
    taps = wd.shape[0]
    reach = before.shape[1]
    span = gm.shape[1]
    inner = wd.shape[1]

    @pl.when(step == 0)
    def _():
        dwn[...] = jnp.zeros_like(dwn) if begun is None else begun[...]
        vecs[...] = jnp.zeros_like(vecs) if begun is None else vecs_begun[...]

    pad[:reach] = before[0]
    pad[reach : reach + span] = gm[0]
    pad[reach + span :] = after[0]
    acc = None
    for k in range(taps):
        at = (taps - 1 - k) * DILATION_SIZE
        term = dot_nt(pad[at : at + span], wd[k])
        acc = term if acc is None else acc + term
    gs[...] = acc

    def one(i, carry):
        gain, shift, bias = carry
        s = pl.ds(i * ROWS, ROWS)
        grad = gs[s, :] * gp2[0, s, :].astype(F32)
        n = n2[0, s, :].astype(F32)
        h = grad * g2[...]
        d = r2[0, s, 0:1] * (
            h - jnp.mean(h, axis=-1, keepdims=True) - n * jnp.mean(h * n, axis=-1, keepdims=True)
        )
        low = d.astype(BF)
        gnl[0, s, :] = low
        return gain + fold(grad * n), shift + fold(grad), bias + fold(low.astype(F32))

    zero = jnp.zeros((8, inner), F32)
    gain, shift, bias = lax.fori_loop(0, span // ROWS, one, (zero, zero, zero), unroll=2)
    vecs[0] += gain
    vecs[1] += shift
    vecs[2] += bias
    dwn[...] += dot_tn(first[0], gnl[0])
    if begun is None:
        return

    @pl.when(step == pl.num_programs(0) - 1)
    def _():
        cut = split_rows(dwn.shape[0])
        deal((dwn.at[:cut],), limits[limits.shape[0] - 1], keep_a, send_a)
        deal((dwn.at[cut:],), limits[limits.shape[0] - 1], keep_b, send_b)


def exit_kernel(limits, gnl, n1, gp1, r1, g1, cot, wn, *refs):
    out, evecs, gf = refs[-3:]
    step = pl.program_id(0)
    span = gnl.shape[1]

    @pl.when(step == 0)
    def _():
        evecs[...] = jnp.zeros_like(evecs) if len(refs) == 3 else refs[1][...]

    gf[...] = dot_nt(gnl[0], wn[...])

    def two(i, _):
        s = pl.ds(i * ROWS, ROWS)
        grad = gf[s, :] * gp1[0, s, :].astype(F32)
        n = n1[0, s, :].astype(F32)
        h = grad * g1[...]
        d = r1[0, s, 0:1] * (
            h - jnp.mean(h, axis=-1, keepdims=True) - n * jnp.mean(h * n, axis=-1, keepdims=True)
        )
        out[0, s, :] = (cot[0, s, :].astype(F32) + d).astype(BF)
        evecs[0] += fold(grad * n)
        evecs[1] += fold(grad)
        return 0

    lax.fori_loop(0, span // ROWS, two, 0, unroll=2)


def call(body, name, part, scalars, ins, outs, scratch, flops=0, nbytes=0, alias=None):
    base, count = part

    def spec(shape, each):
        rest = (0,) * (len(shape) - 1)
        if each is None:
            return pl.BlockSpec(memory_space=pl.ANY)
        if each == "own":
            return pl.BlockSpec((1,) + tuple(shape[1:]), lambda i, *_: (i,) + rest)
        if each:
            return pl.BlockSpec((1,) + tuple(shape[1:]), lambda i, *_: (i + base,) + rest)
        return pl.BlockSpec(tuple(shape), lambda i, *_: (0,) + rest)

    return pl.pallas_call(
        body,
        name=name,
        grid_spec=pltpu.PrefetchScalarGridSpec(
            num_scalar_prefetch=1,
            grid=(count,),
            in_specs=[spec(a.shape, e) for a, e in ins],
            out_specs=[spec(s, e) for s, _, e in outs],
            scratch_shapes=[pltpu.VMEM(s, d) for s, d in scratch],
        ),
        out_shape=[jax.ShapeDtypeStruct(s, d) for s, d, _ in outs],
        compiler_params=pltpu.CompilerParams(vmem_limit_bytes=VMEM),
        cost_estimate=pl.CostEstimate(flops=flops, transcendentals=0, bytes_accessed=nbytes),
        input_output_aliases=alias or {},
    )(scalars, *[a for a, _ in ins])


def halo(cells, width):
    count = lax.axis_size("seq")
    ends = count - 1
    before = lax.ppermute(cells[:, cells.shape[1] - width :], "seq", [(i, i + 1) for i in range(ends)])
    after = lax.ppermute(cells[:, :width], "seq", [(i + 1, i) for i in range(ends)])
    return before, after


def partner(axis, bit):
    count = lax.axis_size(axis)
    return [(i, i ^ (1 << bit)) for i in range(count)]


def bit_of(axis, bit):
    return (lax.axis_index(axis) >> bit) & 1


def hops():
    return [(axis, bit) for axis in ("seq", "item") for bit in range(lax.axis_size(axis).bit_length() - 1)]


def halves(cells, axis, bit):
    half = cells.shape[0] // 2
    mine = bit_of(axis, bit)
    return (
        lax.dynamic_slice_in_dim(cells, mine * half, half, 0),
        lax.dynamic_slice_in_dim(cells, (1 - mine) * half, half, 0),
    )


def phases(keep, send, order):
    sums = yield keep + lax.ppermute(send, order[0][0], partner(*order[0])).astype(F32)
    for hop in order[1:-1]:
        mine, other = halves(sums, *hop)
        sums = yield mine + lax.ppermute(other.astype(BF), hop[0], partner(*hop)).astype(F32)
    low = sums.astype(BF)
    other = lax.ppermute(low, order[-1][0], partner(*order[-1]))
    cells = yield (low.astype(F32) + other.astype(F32)).astype(BF)
    for hop in order[-2::-1]:
        other = lax.ppermute(cells, hop[0], partner(*hop))
        mine = bit_of(*hop) == 0
        cells = yield jnp.concatenate([jnp.where(mine, cells, other), jnp.where(mine, other, cells)])


class Sums:
    def __init__(self):
        self.running = []

    def add(self, *pieces):
        for keep, send, order in pieces:
            work = phases(keep, send, order)
            self.running.append([work, next(work), True])

    def step(self):
        for item in self.running:
            if item[2]:
                try:
                    item[1] = item[0].send(item[1])
                except StopIteration:
                    item[2] = False

    def before(self, value):
        live = [item for item in self.running if item[2]]
        value, states = lax.optimization_barrier((value, [item[1] for item in live]))
        for item, state in zip(live, states):
            item[1] = state
        return value

    def finish(self):
        while any(item[2] for item in self.running):
            self.step()
        return [item[1] for item in self.running]


def total_small(values, order):
    for hop in order:
        values = values + lax.ppermute(values, hop[0], partner(*hop))
    return values


def on_device(tokens, lengths, entry_gain, entry_shift, narrow_weight, narrow_bias, middle_gain, middle_shift,
              dilated_weight, dilated_bias, final_gain, final_shift, widen_weight, widen_bias, out_cotangent):
    seqs, span, width = tokens.shape
    taps, inner, _ = dilated_weight.shape
    reach = (taps - 1) // 2 * DILATION_SIZE
    limits = lengths - lax.axis_index("seq").astype(jnp.int32) * span

    limits = jnp.concatenate([limits, bit_of("seq", 0).astype(jnp.int32).reshape(1)])
    order = hops()
    swapped = [order[0], order[2], order[1]] + order[3:]

    def row(v):
        return v.reshape(1, -1)

    wide = (seqs, span, width)
    slim = (seqs, span, inner)
    stat = (seqs, span, 128)
    rows = seqs * span
    first, n1, gp1, r1, second, n2, gp2, r2 = call(
        entry_kernel, "entry", (0, seqs), limits,
        [(tokens, True), (row(entry_gain), False), (row(entry_shift), False), (narrow_weight, False),
         (row(narrow_bias), False), (row(middle_gain), False), (row(middle_shift), False)],
        [(wide, BF, True), (wide, BF, True), (wide, BF, True), (stat, F32, True),
         (slim, BF, True), (slim, BF, True), (slim, BF, True), (stat, F32, True)],
        [((span, inner), F32)],
        flops=16 * rows * width * inner, nbytes=rows * width * 12,
    )
    before, after = halo(second, reach)
    cut = split_rows(taps * inner)
    half_a = (inner + cut) // 2
    half_b = (inner + taps * inner - cut) // 2
    out, gm, keep_a, send_a, keep_b, send_b, vecs3, wsum = call(
        middle_kernel, "middle", (0, seqs), limits,
        [(tokens, True), (out_cotangent, True), (second, True), (before, True), (after, True),
         (dilated_weight, False), (row(dilated_bias), False), (row(final_gain), False), (row(final_shift), False),
         (widen_weight, False), (row(widen_bias), False)],
        [(wide, BF, True), (slim, BF, True),
         ((half_a, inner), F32, False), ((half_a, inner), BF, False),
         ((half_b, inner), F32, False), ((half_b, inner), BF, False),
         ((3, 8, inner), F32, False), ((8, width), F32, False)],
        [((inner, width), F32), ((taps * inner, inner), F32),
         ((span + 2 * reach, inner), BF), ((span, inner), F32), ((span, inner), BF), ((span, inner), F32),
         ((span, inner), F32), ((span, 128), F32), ((span, inner), F32)],
        flops=16 * rows * width * inner, nbytes=rows * width * 12,
    )
    gbefore, gafter = halo(gm, reach)
    sums = Sums()
    sums.add((keep_a, send_a, order), (keep_b, send_b, swapped))
    cut_c = split_rows(width)
    half_c = cut_c // 2
    half_d = (width - cut_c) // 2
    parts = [(0, seqs // 2), (seqs // 2, seqs - seqs // 2)]
    lows = []
    begun = []
    for part in parts:
        gm = sums.before(gm)
        last = part is parts[-1]
        outs = [((part[1], span, inner), BF, "own"), ((3, 8, inner), F32, False)]
        scratch = [((span + 2 * reach, inner), BF), ((span, inner), F32)]
        if last:
            outs += [((half_c, inner), F32, False), ((half_c, inner), BF, False),
                     ((half_d, inner), F32, False), ((half_d, inner), BF, False)]
            scratch = [((width, inner), F32)] + scratch
        else:
            outs += [((width, inner), F32, False)]
        low, vecs2, *begun = call(
            back_kernel, "back", part, limits,
            [(gm, True), (gbefore, True), (gafter, True), (dilated_weight, False), (n2, True), (gp2, True), (r2, True),
             (row(middle_gain), False), (first, True)] + [(v, False) for v in begun],
            outs, scratch,
            flops=7 * rows * width * inner // 2, nbytes=rows * width * 6,
        )
        begun = begun + [vecs2]
        lows.append(low)
        sums.step()
    keep_c, send_c, keep_d, send_d, _ = begun
    sums.add((keep_c, send_c, order), (keep_d, send_d, swapped))
    tokens_grad = evecs = None
    pieces = max(1, seqs // len(parts) // 2)
    for part, low in zip(parts, lows):
        for at in range(0, part[1], pieces):
            low = sums.before(low)
            begun = [] if evecs is None else [(tokens_grad, None), (evecs, False)]
            here = (part[0] + at, min(pieces, part[1] - at))
            tokens_grad, evecs = call(
                exit_kernel, "exit", here, limits,
                [(low[at : at + here[1]], "own"), (n1, True), (gp1, True), (r1, True), (row(entry_gain), False),
                 (out_cotangent, True), (narrow_weight, False)] + begun,
                [(wide, BF, True), ((2, 8, width), F32, False)],
                [((span, width), F32)],
                flops=rows * width * inner // 2, nbytes=rows * width * 2,
                alias={8: 0} if begun else None,
            )
            sums.step()
    sum_a, sum_b, sum_c, sum_d = sums.finish()
    swd = jnp.concatenate([sum_a[inner:], sum_b[inner:]]).astype(F32).reshape(taps, inner, inner)
    sww = jnp.concatenate([sum_a[:inner], sum_b[:inner]], axis=1).astype(F32)
    swn = jnp.concatenate([sum_c, sum_d]).astype(F32)
    small = jnp.concatenate(
        [evecs.sum(1).reshape(-1), wsum.sum(0), vecs2.sum(1).reshape(-1), vecs3.sum(1).reshape(-1)]
    )
    small = total_small(small, order)
    eg, es, wb = (small[i * width : (i + 1) * width] for i in range(3))
    mg, ms, nb, fg, fs, db = (small[3 * width + i * inner : 3 * width + (i + 1) * inner] for i in range(6))
    return (out, tokens_grad, eg, es, swn, nb, mg, ms, swd, db, fg, fs, sww, wb)


def solution(mesh):
    split = P("item", "seq", None)
    in_specs = (split, P("item")) + (P(),) * 12 + (split,)
    out_specs = (split, split) + (P(),) * 12
    return jax.shard_map(on_device, mesh=mesh, in_specs=in_specs, out_specs=out_specs, check_vma=False)
```

```python
import functools

import jax
import jax.numpy as jnp
from jax import lax
from jax.experimental import pallas as pl
from jax.experimental.pallas import tpu as pltpu
from jax.sharding import PartitionSpec as P

DILATION_SIZE = 64
EPS = 1e-05
BF = jnp.bfloat16
F32 = jnp.float32
ROWS = 16
CHUNK = 32
VMEM = 60 << 20
LOG2E = 1.4426950408889634
SCALE = (0.5 * LOG2E) ** 0.5
BELL = -1.3257480647361593
TERMS = (0.254829592, -0.284496736, 1.421413741, -1.453152027, 1.061405429)


def gelu_parts(z):
    t = 1.0 / (1.0 + (0.3275911 * 0.7071067811865476 / SCALE) * jnp.abs(z))
    bell = jnp.exp2(BELL - z * z)
    scaled = [c * (0.5 / 0.3989422804014327 / SCALE) for c in TERMS]
    poly = scaled[-1]
    for c in scaled[-2::-1]:
        poly = poly * t + c
    tail = poly * t * bell
    cdf = jnp.where(z >= 0, 1.0 / SCALE - tail, tail)
    return cdf, cdf + z * (bell * (1.0 / SCALE / SCALE))


def norm_stats(v):
    mean = jnp.mean(v, axis=-1, keepdims=True)
    c = v - mean
    r = lax.rsqrt(jnp.mean(c * c, axis=-1, keepdims=True) + EPS)
    return c * r, r


def fold(v):
    return jnp.sum(v.reshape(-1, 8, v.shape[-1]), axis=0)


def sweep(limit, span, body, carry, rest):
    count = jnp.clip((limit + CHUNK - 1) // CHUNK, 0, span // CHUNK)

    def one(i, carry):
        for at in range(0, CHUNK, ROWS):
            start = pl.multiple_of(i * CHUNK + at, ROWS)
            keep = start + lax.broadcasted_iota(jnp.int32, (ROWS, 1), 0) < limit
            carry = body(pl.ds(start, ROWS), keep, carry)
        return carry

    def other(i, _):
        rest(pl.ds(pl.multiple_of(i * CHUNK, CHUNK), CHUNK))
        return 0

    carry = lax.fori_loop(0, count, one, carry)
    lax.fori_loop(count, span // CHUNK, other, 0)
    return carry


def blank(width):
    return jnp.zeros((CHUNK, width), BF)


def flat(v):
    return v.reshape(v.shape[0] * v.shape[1], v.shape[2])


def window(pad, at, span):
    return flat(pad[:, at : at + span])


def entry_kernel(limits, tok, ge, wn, gi, first, n1, gp1, r1, second, n2, gp2, r2, narrow, *, base):
    group, span, width = tok.shape
    inner = wn.shape[1]
    for q in range(group):
        limit = limits[base + pl.program_id(0) * group + q]

        def one(s, keep, _):
            n, r = norm_stats(tok[q, s, :].astype(F32))
            z = n * ge[0:1, :] + ge[1:2, :]
            cdf, slope = gelu_parts(z)
            first[q, s, :] = jnp.where(keep, z * cdf, 0.0).astype(BF)
            gp1[q, s, :] = slope.astype(BF)
            n1[q, s, :] = n.astype(BF)
            r1[q, s, :] = jnp.broadcast_to(r, (ROWS, 128))
            return 0

        def clear(s):
            first[q, s, :] = blank(width)

        sweep(limit, span, one, 0, clear)
    narrow[...] = (jnp.dot(flat(first[...]), wn[...], preferred_element_type=F32) + gi[0:1, :]).reshape(narrow.shape)
    for q in range(group):
        limit = limits[base + pl.program_id(0) * group + q]

        def two(s, keep, _):
            n, r = norm_stats(narrow[q, s, :])
            z = n * gi[1:2, :] + gi[2:3, :]
            cdf, slope = gelu_parts(z)
            second[q, s, :] = jnp.where(keep, z * cdf, 0.0).astype(BF)
            gp2[q, s, :] = jnp.where(keep, slope, 0.0).astype(BF)
            n2[q, s, :] = n.astype(BF)
            r2[q, s, :] = jnp.broadcast_to(r, (ROWS, 128))
            return 0

        def clear(s):
            second[q, s, :] = blank(inner)

        sweep(limit, span, two, 0, clear)


def dot_nt(a, b):
    return lax.dot_general(a, b, (((1,), (1,)), ((), ())), preferred_element_type=F32)


def dot_tn(a, b):
    return lax.dot_general(a, b, (((0,), (0,)), ((), ())), preferred_element_type=F32)


def widen_halo(pad, before, own, after):
    reach = before.shape[1]
    span = own.shape[1]
    pad[:, :reach] = before[...]
    pad[:, reach : reach + span] = own[...]
    pad[:, reach + span :] = after[...]


def input_grad(grad, n, r, gain):
    h = grad * gain
    gn = grad * n
    return gn, r * (h - jnp.mean(h, axis=-1, keepdims=True) - n * jnp.mean(gn * gain, axis=-1, keepdims=True))


def middle_kernel(limits, tok, cot, own, before, after, wd, gi, ww, gw,
                  out, gm, dww, vecs, wsum, pad, mixed, third, n3, gp3, r3, gt):
    step = pl.program_id(0)
    taps, inner, _ = wd.shape
    group, span, _ = tok.shape

    @pl.when(step == 0)
    def _():
        dww[...] = jnp.zeros_like(dww)
        vecs[...] = jnp.zeros_like(vecs)
        wsum[...] = jnp.zeros_like(wsum)

    widen_halo(pad, before, own, after)
    acc = gi[0:1, :]
    for k in range(taps):
        acc = acc + jnp.dot(window(pad, k * DILATION_SIZE, span), wd[k], preferred_element_type=F32)
    mixed[...] = acc.reshape(mixed.shape)
    for q in range(group):
        limit = limits[step * group + q]

        def one(s, keep, _):
            n, r = norm_stats(mixed[q, s, :])
            z = n * gi[1:2, :] + gi[2:3, :]
            cdf, slope = gelu_parts(z)
            third[q, s, :] = jnp.where(keep, z * cdf, 0.0).astype(BF)
            gp3[q, s, :] = jnp.where(keep, slope, 0.0)
            n3[q, s, :] = n
            r3[q, s, :] = jnp.broadcast_to(r, (ROWS, 128))
            return 0

        def clear(s):
            third[q, s, :] = blank(inner)

        sweep(limit, span, one, 0, clear)
    lows = flat(third[...])
    cots = flat(cot[...])
    widened = jnp.dot(lows, ww[...], preferred_element_type=F32) + gw[...]
    out[...] = (flat(tok[...]).astype(F32) + widened).astype(BF).reshape(out.shape)
    wsum[...] += fold(cots.astype(F32))
    dww[...] += dot_tn(lows, cots)
    gt[...] = dot_nt(cots, ww[...]).reshape(gt.shape)
    zero = jnp.zeros((8, inner), F32)
    for q in range(group):
        limit = limits[step * group + q]

        def two(s, keep, carry):
            gain, shift, bias = carry
            grad = gt[q, s, :] * gp3[q, s, :]
            gn, d = input_grad(grad, n3[q, s, :], r3[q, s, 0:1], gi[1:2, :])
            low = d.astype(BF)
            gm[q, s, :] = low
            return gain + fold(gn), shift + fold(grad), bias + fold(low.astype(F32))

        def clear(s):
            gm[q, s, :] = blank(inner)

        sums = sweep(limit, span, two, (zero, zero, zero), clear)
        for i in range(3):
            vecs[i] += sums[i]


def taps_kernel(limits, own, before, after, gm, dww, keep_a, send_a, keep_b, send_b, dwd, pad, *, taps):
    step = pl.program_id(0)
    span, inner = own.shape[1:]

    @pl.when(step == 0)
    def _():
        dwd[...] = jnp.zeros_like(dwd)

    widen_halo(pad, before, own, after)
    for k in range(taps):
        dwd[k * inner : (k + 1) * inner] += dot_tn(window(pad, k * DILATION_SIZE, span), flat(gm[...]))

    @pl.when(step == pl.num_programs(0) - 1)
    def _():
        cut = split_rows(taps * inner)
        deal((dww.at[:, :inner], dwd.at[:cut]), limits[limits.shape[0] - 1], keep_a, send_a)
        deal((dww.at[:, inner:], dwd.at[cut:]), limits[limits.shape[0] - 1], keep_b, send_b)


def split_rows(rows):
    return rows // 2 // 128 * 128


def deal(parts, bit, keep, send):
    half = keep.shape[0]

    def put(chosen, target, kind):
        at = 0
        for part in parts:
            low, high = max(at, chosen * half), min(at + part.shape[0], (chosen + 1) * half)
            if low < high:
                target[low - chosen * half : high - chosen * half] = part[low - at : high - at].astype(kind)
            at += part.shape[0]

    for value in (0, 1):

        @pl.when(bit == value)
        def _():
            put(value, keep, F32)
            put(1 - value, send, BF)


def back_kernel(limits, gm, before, after, wd, n2, gp2, r2, gi, first, *refs, base):
    if len(refs) == 5:
        gnl, vecs, dwn, pad, gs = refs
        begun = None
    else:
        begun, vecs_begun, gnl, vecs, keep_a, send_a, keep_b, send_b, dwn, pad, gs = refs
    step = pl.program_id(0)
    taps, inner, _ = wd.shape
    group, span, _ = gm.shape

    @pl.when(step == 0)
    def _():
        dwn[...] = jnp.zeros_like(dwn) if begun is None else begun[...]
        vecs[...] = jnp.zeros_like(vecs) if begun is None else vecs_begun[...]

    widen_halo(pad, before, gm, after)
    acc = None
    for k in range(taps):
        term = dot_nt(window(pad, (taps - 1 - k) * DILATION_SIZE, span), wd[k])
        acc = term if acc is None else acc + term
    gs[...] = acc.reshape(gs.shape)
    zero = jnp.zeros((8, inner), F32)
    for q in range(group):
        limit = limits[base + step * group + q]

        def one(s, keep, carry):
            gain, shift, bias = carry
            grad = gs[q, s, :] * gp2[q, s, :].astype(F32)
            gn, d = input_grad(grad, n2[q, s, :].astype(F32), r2[q, s, 0:1], gi[...])
            low = d.astype(BF)
            gnl[q, s, :] = low
            return gain + fold(gn), shift + fold(grad), bias + fold(low.astype(F32))

        def clear(s):
            gnl[q, s, :] = blank(inner)

        sums = sweep(limit, span, one, (zero, zero, zero), clear)
        for i in range(3):
            vecs[i] += sums[i]
    dwn[...] += dot_tn(flat(first[...]), flat(gnl[...]))
    if begun is None:
        return

    @pl.when(step == pl.num_programs(0) - 1)
    def _():
        cut = split_rows(dwn.shape[0])
        deal((dwn.at[:cut],), limits[limits.shape[0] - 1], keep_a, send_a)
        deal((dwn.at[cut:],), limits[limits.shape[0] - 1], keep_b, send_b)


def exit_kernel(limits, gnl, n1, gp1, r1, ge, cot, wn, *refs, base):
    out, evecs, gf = refs[-3:]
    step = pl.program_id(0)
    group, span, _ = gnl.shape

    @pl.when(step == 0)
    def _():
        evecs[...] = jnp.zeros_like(evecs) if len(refs) == 3 else refs[1][...]

    gf[...] = dot_nt(flat(gnl[...]), wn[...]).reshape(gf.shape)
    for q in range(group):
        limit = limits[base + step * group + q]

        def one(s, keep, _):
            grad = gf[q, s, :] * gp1[q, s, :].astype(F32)
            gn, d = input_grad(grad, n1[q, s, :].astype(F32), r1[q, s, 0:1], ge[...])
            out[q, s, :] = (cot[q, s, :].astype(F32) + d).astype(BF)
            evecs[0] += fold(gn)
            evecs[1] += fold(grad)
            return 0

        def clear(s):
            out[q, s, :] = cot[q, s, :]

        sweep(limit, span, one, 0, clear)


def call(body, name, part, scalars, ins, outs, scratch, flops=0, nbytes=0, alias=None, **static):
    base, count, group = part

    def spec(shape, how):
        rest = (0,) * (len(shape) - 1)
        if how is None:
            return pl.BlockSpec(memory_space=pl.ANY)
        if how == "own":
            return pl.BlockSpec((group,) + tuple(shape[1:]), lambda i, *_: (i,) + rest)
        if how:
            return pl.BlockSpec((group,) + tuple(shape[1:]), lambda i, *_: (i + base // group,) + rest)
        return pl.BlockSpec(tuple(shape), lambda i, *_: (0,) + rest)

    return pl.pallas_call(
        functools.partial(body, **static) if static else body,
        name=name,
        grid_spec=pltpu.PrefetchScalarGridSpec(
            num_scalar_prefetch=1,
            grid=(count // group,),
            in_specs=[spec(a.shape, e) for a, e in ins],
            out_specs=[spec(s, e) for s, _, e in outs],
            scratch_shapes=[pltpu.VMEM(s, d) for s, d in scratch],
        ),
        out_shape=[jax.ShapeDtypeStruct(s, d) for s, d, _ in outs],
        compiler_params=pltpu.CompilerParams(vmem_limit_bytes=VMEM),
        cost_estimate=pl.CostEstimate(flops=flops, transcendentals=0, bytes_accessed=nbytes),
        input_output_aliases=alias or {},
    )(scalars, *[a for a, _ in ins])


def halo(cells, width):
    count = lax.axis_size("seq")
    ends = count - 1
    before = lax.ppermute(cells[:, cells.shape[1] - width :], "seq", [(i, i + 1) for i in range(ends)])
    after = lax.ppermute(cells[:, :width], "seq", [(i + 1, i) for i in range(ends)])
    return before, after


def partner(axis, bit):
    count = lax.axis_size(axis)
    return [(i, i ^ (1 << bit)) for i in range(count)]


def bit_of(axis, bit):
    return (lax.axis_index(axis) >> bit) & 1


def hops():
    return [(axis, bit) for axis in ("seq", "item") for bit in range(lax.axis_size(axis).bit_length() - 1)]


def halves(cells, axis, bit):
    half = cells.shape[0] // 2
    mine = bit_of(axis, bit)
    return (
        lax.dynamic_slice_in_dim(cells, mine * half, half, 0),
        lax.dynamic_slice_in_dim(cells, (1 - mine) * half, half, 0),
    )


def phases(keep, send, order):
    sums = yield keep + lax.ppermute(send, order[0][0], partner(*order[0])).astype(F32)
    for hop in order[1:-1]:
        mine, other = halves(sums, *hop)
        sums = yield mine + lax.ppermute(other.astype(BF), hop[0], partner(*hop)).astype(F32)
    low = sums.astype(BF)
    other = lax.ppermute(low, order[-1][0], partner(*order[-1]))
    cells = yield (low.astype(F32) + other.astype(F32)).astype(BF)
    for hop in order[-2::-1]:
        other = lax.ppermute(cells, hop[0], partner(*hop))
        mine = bit_of(*hop) == 0
        cells = yield jnp.concatenate([jnp.where(mine, cells, other), jnp.where(mine, other, cells)])


class Sums:
    def __init__(self):
        self.running = []

    def add(self, *pieces):
        for keep, send, order in pieces:
            work = phases(keep, send, order)
            self.running.append([work, next(work), True])

    def step(self):
        for item in self.running:
            if item[2]:
                try:
                    item[1] = item[0].send(item[1])
                except StopIteration:
                    item[2] = False

    def before(self, value):
        live = [item for item in self.running if item[2]]
        value, states = lax.optimization_barrier((value, [item[1] for item in live]))
        for item, state in zip(live, states):
            item[1] = state
        return value

    def finish(self):
        while any(item[2] for item in self.running):
            self.step()
        return [item[1] for item in self.running]


def total_small(values, order):
    for hop in order:
        values = values + lax.ppermute(values, hop[0], partner(*hop))
    return values


def on_device(tokens, lengths, entry_gain, entry_shift, narrow_weight, narrow_bias, middle_gain, middle_shift,
              dilated_weight, dilated_bias, final_gain, final_shift, widen_weight, widen_bias, out_cotangent):
    seqs, span, width = tokens.shape
    taps, inner, _ = dilated_weight.shape
    reach = (taps - 1) // 2 * DILATION_SIZE
    limits = lengths - lax.axis_index("seq").astype(jnp.int32) * span

    limits = jnp.concatenate([limits, bit_of("seq", 0).astype(jnp.int32).reshape(1)])
    order = hops()
    swapped = [order[0], order[2], order[1]] + order[3:]

    group = 2 if seqs % 2 == 0 else 1
    everyone = (0, seqs, group)
    ge = jnp.stack([entry_gain, entry_shift]) * SCALE
    gi = jnp.stack([narrow_bias, middle_gain * SCALE, middle_shift * SCALE])
    gm3 = jnp.stack([dilated_bias, final_gain * SCALE, final_shift * SCALE])
    wide = (seqs, span, width)
    slim = (seqs, span, inner)
    edge = (group, span + 2 * reach, inner)
    rows = seqs * span
    work = rows * width * inner

    def entry(part):
        base, count, _ = part
        here = (count, span)
        return call(
            entry_kernel, "entry", part, limits,
            [(tokens, True), (ge, False), (narrow_weight, False), (gi, False)],
            [(here + (width,), BF, "own")] * 3 + [(here + (128,), F32, "own")]
            + [(here + (inner,), BF, "own")] * 3 + [(here + (128,), F32, "own")],
            [((group, span, inner), F32)],
            flops=16 * work, nbytes=rows * width * 12, base=base,
        )

    first, n1, gp1, r1, second, n2, gp2, r2 = entry(everyone)
    before, after = halo(second, reach)
    out, gm, dww, vecs3, wsum = call(
        middle_kernel, "middle", everyone, limits,
        [(tokens, True), (out_cotangent, True), (second, True), (before, True), (after, True),
         (dilated_weight, False), (gm3, False), (widen_weight, False), (widen_bias.reshape(1, -1), False)],
        [(wide, BF, True), (slim, BF, True), ((inner, width), F32, False),
         ((3, 8, inner), F32, False), ((8, width), F32, False)],
        [(edge, BF), ((group, span, inner), F32), ((group, span, inner), BF), ((group, span, inner), F32),
         ((group, span, inner), F32), ((group, span, 128), F32), ((group, span, inner), F32)],
        flops=16 * work, nbytes=rows * width * 12,
    )
    gbefore, gafter = halo(gm, reach)
    cut = split_rows(taps * inner)
    half_a = (inner + cut) // 2
    half_b = (inner + taps * inner - cut) // 2
    keep_a, send_a, keep_b, send_b = call(
        taps_kernel, "taps", everyone, limits,
        [(second, True), (before, True), (after, True), (gm, True), (dww, False)],
        [((half_a, inner), F32, False), ((half_a, inner), BF, False),
         ((half_b, inner), F32, False), ((half_b, inner), BF, False)],
        [((taps * inner, inner), F32), (edge, BF)],
        flops=5 * work, nbytes=rows * width * 4, taps=taps,
    )
    sums = Sums()
    sums.add((keep_a, send_a, order), (keep_b, send_b, swapped))
    cut_c = split_rows(width)
    half_c = cut_c // 2
    half_d = (width - cut_c) // 2
    middle = seqs // (2 * group) * group
    parts = [(0, middle, group), (middle, seqs - middle, group)] if middle else [everyone, (seqs, 0, group)]
    lows = []
    begun = []
    for part in parts:
        gm = sums.before(gm)
        last = part is parts[-1]
        outs = [((part[1], span, inner), BF, "own"), ((3, 8, inner), F32, False)]
        scratch = [(edge, BF), ((group, span, inner), F32)]
        if last:
            outs += [((half_c, inner), F32, False), ((half_c, inner), BF, False),
                     ((half_d, inner), F32, False), ((half_d, inner), BF, False)]
            scratch = [((width, inner), F32)] + scratch
        else:
            outs += [((width, inner), F32, False)]
        low, vecs2, *begun = call(
            back_kernel, "back", part, limits,
            [(gm, True), (gbefore, True), (gafter, True), (dilated_weight, False), (n2, True), (gp2, True), (r2, True),
             (gi[1:2], False), (first, True)] + [(v, False) for v in begun],
            outs, scratch,
            flops=7 * work // 2, nbytes=rows * width * 6, base=part[0],
        )
        begun = begun + [vecs2]
        lows.append(low)
        sums.step()
    keep_c, send_c, keep_d, send_d, _ = begun
    sums.add((keep_c, send_c, order), (keep_d, send_d, swapped))
    tokens_grad = evecs = None
    for part, low in zip(parts, lows):
        for at in range(0, part[1], group):
            low = sums.before(low)
            begun = [] if evecs is None else [(tokens_grad, None), (evecs, False)]
            here = (part[0] + at, group, group)
            tokens_grad, evecs = call(
                exit_kernel, "exit", here, limits,
                [(low[at : at + group], "own"), (n1, True), (gp1, True), (r1, True), (ge[0:1], False),
                 (out_cotangent, True), (narrow_weight, False)] + begun,
                [(wide, BF, True), ((2, 8, width), F32, False)],
                [((group, span, width), F32)],
                flops=work // 2, nbytes=rows * width * 2,
                alias={8: 0} if begun else None, base=here[0],
            )
            sums.step()
    sum_a, sum_b, sum_c, sum_d = sums.finish()
    swd = jnp.concatenate([sum_a[inner:], sum_b[inner:]]).astype(F32).reshape(taps, inner, inner)
    sww = jnp.concatenate([sum_a[:inner], sum_b[:inner]], axis=1).astype(F32)
    swn = jnp.concatenate([sum_c, sum_d]).astype(F32)
    evecs, vecs2, vecs3 = (v.sum(1) for v in (evecs, vecs2, vecs3))
    small = jnp.concatenate(
        [evecs[0] * SCALE, evecs[1] * SCALE, wsum.sum(0), vecs2[0] * SCALE, vecs2[1] * SCALE, vecs2[2],
         vecs3[0] * SCALE, vecs3[1] * SCALE, vecs3[2]]
    )
    small = total_small(small, order)
    eg, es, wb = (small[i * width : (i + 1) * width] for i in range(3))
    mg, ms, nb, fg, fs, db = (small[3 * width + i * inner : 3 * width + (i + 1) * inner] for i in range(6))
    return (out, tokens_grad, eg, es, swn, nb, mg, ms, swd, db, fg, fs, sww, wb)


def solution(mesh):
    split = P("item", "seq", None)
    in_specs = (split, P("item")) + (P(),) * 12 + (split,)
    out_specs = (split, split) + (P(),) * 12
    return jax.shard_map(on_device, mesh=mesh, in_specs=in_specs, out_specs=out_specs, check_vma=False)
```
